128 devices in a mesh: dp: 8 (over x, y_hi), blk: 16 (over z, y_lo, core).
Axes of the slice: x: 4, y: 4 (y_hi: 2, y_lo: 2; y = y_hi * 2 + y_lo), z: 4, core: 2. Of those that a mesh axis runs over, the one named last changes fastest.
Arguments:
- tokens: bfloat16 [5120, 3072], P(('dp', 'blk')), may hold values from -24 to 24
- expert_ids: int32 [5120, 2], P(('dp', 'blk')), may hold values from 0 to 7, as said below
- route_probs: float32 [5120, 2], P(('dp', 'blk')), may hold values from 0.2 to 1
- scale_exps: int32 [3], replicated, may hold values from -2 to 2
- w_gate: bfloat16 [3072, 8192], P(None, 'blk'), may hold values from -0.109375 to 0.109375
- w_up: bfloat16 [3072, 8192], P(None, 'blk'), may hold values from -0.109375 to 0.109375
- w_down: bfloat16 [8192, 3072], P('blk'), may hold values from -0.0625 to 0.0625
- out_grad: bfloat16 [5120, 3072], P(('dp', 'blk')), may hold values from -24 to 24
Outputs:
- mixed: bfloat16 [5120, 3072], P(('dp', 'blk'))
- input_grad: bfloat16 [5120, 3072], P(('dp', 'blk'))
- grad_gate: bfloat16 [3072, 8192], P('dp', 'blk')
- grad_up: bfloat16 [3072, 8192], P('dp', 'blk')
- grad_down: bfloat16 [8192, 3072], P('blk', 'dp')
The draws below stay inside these ranges and needn't reach their ends.
Inputs may be any that keep to these rules, and one draw needn't show every extreme that they name: `expert_ids`: the tokens are those dispatched to expert 0: each row names expert 0 and one other expert; the layer computes expert 0.
All inputs are finite; a program needn't handle non-finite values.
Results may differ from the reference program's by a relative error of at most 0.019.
Values may be sent and summed in bfloat16 or wider, within the bound.
No kernel may reach another device: no remote copies, remote signals or barrier semaphores. Data moves between devices by JAX's collectives and lax.ppermute only.
A program may use at most 128 MiB of HBM per device.

```python
import jax
import jax.numpy as jnp

D = 3072
FF = 8192
EXPERTS = 8
TOP = 2
TOKENS = 5120


def draw_expert_ids(key, part):
    other_key = jax.random.fold_in(key, 11)
    place_key = jax.random.fold_in(key, 23)
    others = jax.random.randint(other_key, (TOKENS,), 1, EXPERTS, dtype=jnp.int32)
    others = others.at[0:EXPERTS - 1].set(jnp.arange(1, EXPERTS, dtype=jnp.int32))
    placed = jax.random.randint(place_key, (TOKENS,), 0, 2, dtype=jnp.int32)
    zeros = jnp.zeros((TOKENS,), jnp.int32)
    first = jnp.where(placed == 1, others, zeros)
    second = jnp.where(placed == 1, zeros, others)
    return jnp.stack([first, second], axis=1).astype(jnp.int32)


def with_spikes(array, key, source, target, shards_of, factor):
    def block_of(dim):
        return (jnp.arange(array.shape[dim]) // (array.shape[dim] // shards_of)).reshape((-1,) + (1,) * (array.ndim - 1 - dim))

    near = jax.random.permutation(key, shards_of)[block_of(target)]
    far = (block_of(target) + shards_of // 2) % shards_of
    return jnp.where((block_of(source) == near) | (block_of(source) == far), factor * array, array)


def levels(stream_key, extent, shards, low, top_value):
    loudness, own = 1.0, jax.random.fold_in(stream_key, 6)
    for axis_at, parts in shards:
        draws = jnp.exp(jax.random.uniform(jax.random.fold_in(own, axis_at), (parts,), jnp.float32, low / len(shards), top_value / len(shards)))
        loudness = loudness * jnp.repeat(draws, extent[axis_at] // parts).reshape([-1 if axis == axis_at else 1 for axis in range(len(extent))])
    return loudness


def bell_draw(own_key, shape, scale, limit, shards=(), held_as=jnp.bfloat16):
    level = levels(own_key, shape, shards, -0.22, 0.18) if shards else 1.0
    array = jax.random.normal(own_key, shape, jnp.float32) * scale * level
    return jnp.minimum(jnp.maximum(array, -limit), limit).astype(held_as)


def bell_draw_with(own_key, extent, width, bound, split, heavy, kind=jnp.bfloat16):
    array = width * jax.random.normal(own_key, extent, jnp.float32)
    if split:
        array = array * levels(own_key, extent, split, -0.22, 0.18)
    return jnp.clip(with_spikes(array, jax.random.fold_in(own_key, 3), *heavy), -bound, bound).astype(kind)


def setup_inputs(seed: int = 0) -> dict:
    seeds = jax.random.split(jax.random.key(seed), 9)
    tokens = bell_draw_with(seeds[0], (TOKENS, D), 1.0, 24.0, ((0, 128),), (0, 1, 128, 5.5))
    expert_ids = draw_expert_ids(jax.random.fold_in(seeds[8], 71), 0)
    route_probs = jnp.clip(0.2 + 0.8 * jax.random.uniform(seeds[2], (TOKENS, TOP), jnp.float32) ** levels(seeds[2], (TOKENS, TOP), ((0, 128),), -0.2, 0.2), 0.2, 1.0)
    scale_exps = jax.random.randint(seeds[3], (3,), -2, 3).astype(jnp.int32)
    w_gate = bell_draw(seeds[4], (D, FF), D ** -0.5, 0.109375, ((1, 16),))
    w_up = bell_draw(seeds[5], (D, FF), D ** -0.5, 0.109375, ((1, 16),))
    w_down = bell_draw(seeds[6], (FF, D), FF ** -0.5, 0.0625, ((0, 16),))
    out_grad = bell_draw_with(seeds[7], (TOKENS, D), 1.0, 24.0, ((0, 128),), (0, 1, 128, 5.5))
    return {"tokens": tokens, "expert_ids": expert_ids, "route_probs": route_probs, "scale_exps": scale_exps, "w_gate": w_gate, "w_up": w_up, "w_down": w_down, "out_grad": out_grad}


def reference(tokens, expert_ids, route_probs, scale_exps, w_gate, w_up, w_down, out_grad):
    scales = jnp.exp2(scale_exps.astype(jnp.float32))
    combine = jnp.sum(jnp.where(expert_ids == 0, route_probs, jnp.zeros_like(route_probs)), axis=1)[:, None]
    gate_pre = jnp.dot(tokens, w_gate, preferred_element_type=jnp.float32) * scales[0]
    up_pre = jnp.dot(tokens, w_up, preferred_element_type=jnp.float32) * scales[1]
    sigmoid_gate = jax.nn.sigmoid(gate_pre)
    hidden = (gate_pre * sigmoid_gate * up_pre).astype(jnp.bfloat16)
    expert_out = jnp.dot(hidden, w_down, preferred_element_type=jnp.float32) * scales[2]
    mixed = (combine * expert_out).astype(jnp.bfloat16)
    scaled = (combine * out_grad.astype(jnp.float32)).astype(jnp.bfloat16)
    d_hidden = jnp.dot(scaled, w_down.T, preferred_element_type=jnp.float32) * scales[2]
    d_gate = (d_hidden * up_pre * sigmoid_gate * (1.0 + gate_pre * (1.0 - sigmoid_gate))).astype(jnp.bfloat16)
    d_up = (d_hidden * gate_pre * sigmoid_gate).astype(jnp.bfloat16)
    input_grad = (jnp.dot(d_gate, w_gate.T, preferred_element_type=jnp.float32) * scales[0]
                  + jnp.dot(d_up, w_up.T, preferred_element_type=jnp.float32) * scales[1]).astype(jnp.bfloat16)
    grad_gate = (jnp.dot(tokens.T, d_gate, preferred_element_type=jnp.float32) * scales[0]).astype(jnp.bfloat16)
    grad_up = (jnp.dot(tokens.T, d_up, preferred_element_type=jnp.float32) * scales[1]).astype(jnp.bfloat16)
    grad_down = (jnp.dot(hidden.T, scaled, preferred_element_type=jnp.float32) * scales[2]).astype(jnp.bfloat16)
    return (mixed, input_grad, grad_gate, grad_up, grad_down)
```

```python
import jax
import jax.numpy as jnp
import numpy as np
from jax import lax
from jax.experimental import pallas as pl
from jax.experimental.pallas import tpu as pltpu
from jax.sharding import PartitionSpec as P

BF16 = jnp.bfloat16
F32 = jnp.float32


GRAY = {0: (0, 0), 1: (1, 0), 2: (1, 1), 3: (0, 1)}
UNGRAY = {uv: x for x, uv in GRAY.items()}


def blk_perm(dz, dyl, dcore):
    pairs = []
    for b in range(16):
        z, yl, core = b // 4, (b // 2) % 2, b % 2
        pairs.append((b, ((z + dz) % 4) * 4 + (yl ^ dyl) * 2 + (core ^ dcore)))
    return pairs


def dp_flip(du, dv, ds):
    pairs = []
    for d in range(8):
        u, v = GRAY[d // 2]
        pairs.append((d, UNGRAY[(u ^ du, v ^ dv)] * 2 + ((d % 2) ^ ds)))
    return pairs


def owner_table():
    rows = np.zeros((8, 8), np.int32)
    for bits in range(8):
        for d, owner in dp_flip(bits >> 2, (bits >> 1) & 1, bits & 1):
            rows[d, bits] = owner
    return rows


def send(value, dz=0, dyl=0, dcore=0):
    return lax.ppermute(value, "blk", blk_perm(dz, dyl, dcore))


def swap(value, du=0, dv=0, ds=0):
    return lax.ppermute(value, "dp", dp_flip(du, dv, ds))


def gather_blk(mine):
    block = jnp.concatenate([mine, send(mine, dyl=1)], axis=0)
    before = send(block, dz=1)
    after = send(block, dz=-1)
    half = mine.shape[0]
    far = jnp.concatenate([send(before[:half], dz=1), send(after[half:], dz=-1)], axis=0)
    pieces = [block, after, far, before]
    return jnp.concatenate(pieces + [send(piece, dcore=1) for piece in pieces], axis=0)


def scatter_blk(own, other):
    own = own + send(other, dcore=1).astype(F32)
    n = own.shape[0] // 8
    rows = [own[i * n : (i + 1) * n] for i in range(8)]
    from_before = send(rows[4].astype(BF16), dz=1)
    from_after = send(rows[5].astype(BF16), dz=-1)
    after = jnp.concatenate([rows[2] + from_before.astype(F32), rows[3]], axis=0).astype(BF16)
    before = jnp.concatenate([rows[6], rows[7] + from_after.astype(F32)], axis=0).astype(BF16)
    got = send(after, dz=1).astype(F32) + send(before, dz=-1).astype(F32)
    keep = rows[0] + got[:n]
    out = (rows[1] + got[n:]).astype(BF16)
    return keep + send(out, dyl=1).astype(F32)


def wgrad_body(table, left, right, send_a, keep_a, send_b, keep_b, left_t):
    step = pl.program_id(0)

    @pl.when(step == 0)
    def _():
        left_t[...] = left[...].T

    half = left_t.shape[0] // 2
    top = jnp.dot(left_t[0:half, :], right[...], preferred_element_type=F32)

    @pl.when(step < 4)
    def _():
        send_a[...] = top.astype(BF16)

    @pl.when(step >= 4)
    def _():
        keep_a[...] = top

    low = jnp.dot(left_t[half:, :], right[...], preferred_element_type=F32)

    @pl.when(step % 4 >= 2)
    def _():
        send_b[...] = low.astype(BF16)

    @pl.when(step % 4 < 2)
    def _():
        keep_b[...] = low


def wgrad(left, right, table):
    rows, ff = left.shape
    chunk = right.shape[1] // 8
    half = ff // 2

    def chunk_of(i, table):
        return 0, table[lax.rem(i + 4, 8)]

    def keep_b_at(i, table):
        return 0, jnp.where(i < 4, jnp.minimum(i, 1), jnp.minimum(i - 2, 3))

    def send_b_at(i, table):
        return 0, jnp.where(i < 4, jnp.maximum(i - 2, 0), jnp.maximum(i - 4, 1))

    return pl.pallas_call(
        wgrad_body,
        grid_spec=pltpu.PrefetchScalarGridSpec(
            num_scalar_prefetch=1,
            grid=(8,),
            in_specs=[
                pl.BlockSpec((rows, ff), lambda i, table: (0, 0)),
                pl.BlockSpec((rows, chunk), chunk_of),
            ],
            out_specs=[
                pl.BlockSpec((half, chunk), lambda i, table: (0, jnp.minimum(i, 3))),
                pl.BlockSpec((half, chunk), lambda i, table: (0, jnp.maximum(i - 4, 0))),
                pl.BlockSpec((half, chunk), send_b_at),
                pl.BlockSpec((half, chunk), keep_b_at),
            ],
            scratch_shapes=[pltpu.VMEM((ff, rows), BF16)],
        ),
        out_shape=[
            jax.ShapeDtypeStruct((half, 4 * chunk), BF16),
            jax.ShapeDtypeStruct((half, 4 * chunk), F32),
            jax.ShapeDtypeStruct((half, 4 * chunk), BF16),
            jax.ShapeDtypeStruct((half, 4 * chunk), F32),
        ],
        cost_estimate=pl.CostEstimate(
            flops=2 * rows * ff * right.shape[1],
            transcendentals=0,
            bytes_accessed=2 * rows * (ff + right.shape[1]) + 6 * ff * right.shape[1] // 2,
        ),
        name="wgrad",
    )(table, left, right)


def scatter_dp(parts, scale):
    send_a, keep_a, send_b, keep_b = parts
    n = send_a.shape[1] // 4
    got_a = swap(send_a, du=1)
    got_b = swap(send_b, dv=1)
    out_a = (keep_a[:, 2 * n :] + got_a[:, 2 * n :].astype(F32)).astype(BF16)
    out_b = (keep_b[:, : 2 * n] + got_b[:, : 2 * n].astype(F32)).astype(BF16)
    two_a = swap(out_a, dv=1)
    two_b = swap(out_b, du=1)
    own_a = keep_a[:, : 2 * n] + got_a[:, : 2 * n].astype(F32) + two_a.astype(F32)
    own_b = keep_b[:, 2 * n :] + got_b[:, 2 * n :].astype(F32) + two_b.astype(F32)
    last = jnp.concatenate([own_a[:, n:], own_b[:, n:]], axis=0).astype(BF16)
    first = jnp.concatenate([own_a[:, :n], own_b[:, :n]], axis=0)
    return (first + swap(last, ds=1).astype(F32)) * scale


def contract_cols(left, right):
    return lax.dot_general(left, right, (((1,), (1,)), ((), ())), preferred_element_type=F32)


def local(tokens, expert_ids, route_probs, scale_exps, w_gate, w_up, w_down, out_grad):
    scales = jnp.exp2(scale_exps.astype(F32))
    combine = jnp.sum(jnp.where(expert_ids == 0, route_probs, jnp.zeros_like(route_probs)), axis=1)[
        :, None
    ]
    table = jnp.asarray(owner_table())[lax.axis_index("dp")]
    scaled = (combine * out_grad.astype(F32)).astype(BF16)
    all_tokens = gather_blk(tokens)
    all_scaled = gather_blk(scaled)
    gate_pre = jnp.dot(all_tokens, w_gate, preferred_element_type=F32) * scales[0]
    up_pre = jnp.dot(all_tokens, w_up, preferred_element_type=F32) * scales[1]
    sig = jax.nn.sigmoid(gate_pre)
    hidden = (gate_pre * sig * up_pre).astype(BF16)
    half = hidden.shape[0] // 2

    other = jnp.dot(hidden[half:], w_down, preferred_element_type=F32).astype(BF16)
    own = jnp.dot(hidden[:half], w_down, preferred_element_type=F32)
    expert_out = scatter_blk(own, other) * scales[2]
    mixed = (combine * expert_out).astype(BF16)

    grad_down = scatter_dp(wgrad(hidden, all_scaled, table), scales[2])

    d_hidden = contract_cols(all_scaled, w_down) * scales[2]
    d_gate = (d_hidden * up_pre * sig * (1.0 + gate_pre * (1.0 - sig))).astype(BF16)
    d_up = (d_hidden * gate_pre * sig).astype(BF16)
    grad_gate = scatter_dp(wgrad(d_gate, all_tokens, table), scales[0])
    grad_up = scatter_dp(wgrad(d_up, all_tokens, table), scales[1])

    def back(rows):
        return (
            contract_cols(d_gate[rows], w_gate) * scales[0]
            + contract_cols(d_up[rows], w_up) * scales[1]
        )

    input_grad = scatter_blk(back(slice(0, half)), back(slice(half, None)).astype(BF16))
    return (
        mixed,
        input_grad.astype(BF16),
        grad_gate.T.astype(BF16),
        grad_up.T.astype(BF16),
        grad_down.astype(BF16),
    )


def solution(mesh):
    return jax.shard_map(
        local,
        mesh=mesh,
        in_specs=(
            P(("dp", "blk"), None),
            P(("dp", "blk"), None),
            P(("dp", "blk"), None),
            P(),
            P(None, "blk"),
            P(None, "blk"),
            P("blk", None),
            P(("dp", "blk"), None),
        ),
        out_specs=(
            P(("dp", "blk"), None),
            P(("dp", "blk"), None),
            P("dp", "blk"),
            P("dp", "blk"),
            P("blk", "dp"),
        ),
        check_vma=False,
    )
```

```python
import jax
import jax.numpy as jnp
import numpy as np
from jax import lax
from jax.experimental import pallas as pl
from jax.experimental.pallas import tpu as pltpu
from jax.sharding import PartitionSpec as P

BF16 = jnp.bfloat16
F32 = jnp.float32

VMEM = pl.BlockSpec(memory_space=pltpu.VMEM)
SMEM = pl.BlockSpec(memory_space=pltpu.SMEM)
HBM = pl.BlockSpec(memory_space=pl.ANY)
GRANT = pltpu.CompilerParams(vmem_limit_bytes=14 * 2**20)


GRAY = {0: (0, 0), 1: (1, 0), 2: (1, 1), 3: (0, 1)}
UNGRAY = {uv: x for x, uv in GRAY.items()}


def blk_flip(dza, dzb, dyl, dcore):
    pairs = []
    for b in range(16):
        (za, zb), yl, core = GRAY[b // 4], (b // 2) % 2, b % 2
        z = UNGRAY[(za ^ dza, zb ^ dzb)]
        pairs.append((b, z * 4 + (yl ^ dyl) * 2 + (core ^ dcore)))
    return pairs


def dp_flip(du, dv, ds):
    pairs = []
    for d in range(8):
        u, v = GRAY[d // 2]
        pairs.append((d, UNGRAY[(u ^ du, v ^ dv)] * 2 + ((d % 2) ^ ds)))
    return pairs


def place_table():
    rows = np.zeros((8, 5), np.int32)
    for bits in range(4):
        for d, owner in dp_flip(bits >> 1, bits & 1, 0):
            rows[d, bits] = owner // 2
    rows[:, 4] = np.arange(8) % 2
    return rows


def send(value, dza=0, dzb=0, dyl=0, dcore=0):
    return lax.ppermute(value, "blk", blk_flip(dza, dzb, dyl, dcore))


def swap(value, du=0, dv=0, ds=0):
    return lax.ppermute(value, "dp", dp_flip(du, dv, ds))


def gather_blk(mine):
    beside = send(mine, dyl=1)
    a = send(mine, dza=1)
    b = send(mine, dzb=1)
    far = send(mine, dza=1, dzb=1)
    a_beside = send(beside, dza=1)
    b_beside = send(beside, dzb=1)
    far_beside = send(far, dyl=1)
    pieces = [mine, beside, b, b_beside, a, a_beside, far, far_beside]
    return pieces + [send(piece, dcore=1) for piece in pieces]


def total(*parts):
    return sum(part.astype(F32) for part in parts)


def scatter_blk(own, other):
    parts = [own, send(other, dcore=1)]
    for flip in ({"dza": 1}, {"dzb": 1}, {"dyl": 1}):
        half = parts[0].shape[0] // 2
        out = total(*(part[half:] for part in parts)).astype(BF16)
        parts = [part[:half] for part in parts] + [send(out, **flip)]
    return total(*parts)


def merge_rows(own, got):
    rows, d = own.shape
    n = rows // 8

    def body(own, got, near, far_a, far_b):
        near[...] = total(own[: 6 * n], got[: 6 * n]).astype(BF16)
        far_a[...] = total(own[6 * n : 7 * n], got[6 * n : 7 * n]).astype(BF16)
        far_b[...] = total(own[7 * n :], got[7 * n :]).astype(BF16)

    return pl.pallas_call(
        body,
        in_specs=[VMEM] * 2,
        out_specs=[VMEM] * 3,
        out_shape=[pltpu.VMEM((count * n, d), BF16) for count in (6, 1, 1)],
        cost_estimate=pl.CostEstimate(
            flops=rows * d, transcendentals=0, bytes_accessed=6 * rows * d
        ),
        compiler_params=GRANT,
    )(own, got)


def scatter_blk_both(own, other):
    got = send(other, dcore=1)
    n = own.shape[0] // 8
    near, far_a, far_b = merge_rows(own, got)
    rows = [near[i * n : (i + 1) * n] for i in range(6)]
    from_a = send(far_a, dza=1)
    from_b = send(far_b, dzb=1)
    b = jnp.concatenate([total(rows[2], from_a), total(rows[3])], axis=0).astype(BF16)
    a = jnp.concatenate([total(rows[4]), total(rows[5], from_b)], axis=0).astype(BF16)
    got_b = send(b, dzb=1)
    got_a = send(a, dza=1)
    out = total(rows[1], got_b[n:], got_a[n:]).astype(BF16)
    last = send(out, dyl=1)
    return total(rows[0], got_b[:n], got_a[:n], last)


def start_copies(pieces, target, sems):
    copies, at = [], 0
    for i, piece in enumerate(pieces):
        copies.append(
            pltpu.make_async_copy(piece, target.at[pl.ds(at, piece.shape[0])], sems.at[i])
        )
        at += piece.shape[0]
    for copy in copies:
        copy.start()
    return copies


def wgrad_cost(rows, ff, d):
    return pl.CostEstimate(
        flops=2 * rows * ff * d, transcendentals=0, bytes_accessed=2 * (rows * (ff + d) + ff * d)
    )


def wgrad_join(table, left, pieces):
    rows, ff = left.shape
    d = pieces[0].shape[1]
    n = len(pieces)

    def body(table, left, *refs):
        ins, (right, *outs), (left_t, sems) = refs[:n], refs[n : n + 5], refs[n + 5 :]
        copies = start_copies(ins, right, sems)
        left_t[...] = left[...].T
        for copy in copies:
            copy.wait()
        cut_x(table, left_t, right, *outs)

    part = pltpu.VMEM((ff // 2, d // 2), BF16)
    return pl.pallas_call(
        body,
        in_specs=[SMEM, VMEM] + [HBM] * n,
        out_specs=[VMEM] * 5,
        out_shape=[pltpu.VMEM((rows, d), BF16)] + [part] * 4,
        scratch_shapes=[pltpu.VMEM((ff, rows), BF16), pltpu.SemaphoreType.DMA((n,))],
        cost_estimate=wgrad_cost(rows, ff, d),
        compiler_params=GRANT,
    )(table, left, *pieces)


def chunk(right, table, j, wide):
    return right[:, pl.ds(pl.multiple_of(table[j] * wide, wide), wide)]


def cut_x(table, left_t, right, send_a, keep_a, send_b, keep_b):
    half, wide = left_t.shape[0] // 2, right.shape[1] // 4
    for j in range(4):
        u, v = j >> 1, j & 1
        value = jnp.dot(
            left_t[...], chunk(right, table, j, wide), preferred_element_type=F32
        ).astype(BF16)
        to_a = send_a if u else keep_a
        to_b = send_b if v else keep_b
        to_a[:, v * wide : (v + 1) * wide] = value[:half]
        to_b[:, u * wide : (u + 1) * wide] = value[half:]


def wgrad_x(table, left, right):
    rows, ff = left.shape
    d = right.shape[1]

    def body(table, left, right, send_a, keep_a, send_b, keep_b, left_t):
        left_t[...] = left[...].T
        cut_x(table, left_t, right, send_a, keep_a, send_b, keep_b)

    return pl.pallas_call(
        body,
        in_specs=[SMEM, VMEM, VMEM],
        out_specs=[VMEM] * 4,
        out_shape=[pltpu.VMEM((ff // 2, d // 2), BF16)] * 4,
        scratch_shapes=[pltpu.VMEM((ff, rows), BF16)],
        cost_estimate=wgrad_cost(rows, ff, d),
        compiler_params=GRANT,
    )(table, left, right)


def wgrad_y(table, left, right):
    rows, ff = left.shape
    d = right.shape[1]
    wide = d // 4
    n = wide // 2

    def body(table, left, right, out, keep, left_t):
        left_t[...] = left[...].T
        for j in range(4):
            cols = slice(j * n, (j + 1) * n)
            value = jnp.dot(
                left_t[...], chunk(right, table, j, wide), preferred_element_type=F32
            ).astype(BF16)

            @pl.when(table[4] == 0)
            def _():
                keep[:, cols] = value[:, :n]
                out[:, cols] = value[:, n:]

            @pl.when(table[4] != 0)
            def _():
                out[:, cols] = value[:, :n]
                keep[:, cols] = value[:, n:]

    return pl.pallas_call(
        body,
        in_specs=[SMEM, VMEM, VMEM],
        out_specs=[VMEM] * 2,
        out_shape=[pltpu.VMEM((ff, d // 2), BF16)] * 2,
        scratch_shapes=[pltpu.VMEM((ff, rows), BF16)],
        cost_estimate=wgrad_cost(rows, ff, d),
        compiler_params=GRANT,
    )(table, left, right)


def cut_sum(keep, got):
    half, n = keep.shape[0] // 2, keep.shape[1] // 4

    def body(keep, got, send_a, keep_a, send_b, keep_b):
        for j in range(4):
            u, v = j >> 1, j & 1
            cols = slice(j * n, (j + 1) * n)
            value = total(keep[:, cols], got[:, cols]).astype(BF16)
            to_a = send_a if u else keep_a
            to_b = send_b if v else keep_b
            to_a[:, v * n : (v + 1) * n] = value[:half]
            to_b[:, u * n : (u + 1) * n] = value[half:]

    return pl.pallas_call(
        body,
        in_specs=[VMEM] * 2,
        out_specs=[VMEM] * 4,
        out_shape=[pltpu.VMEM((half, 2 * n), BF16)] * 4,
        cost_estimate=pl.CostEstimate(
            flops=keep.size, transcendentals=0, bytes_accessed=6 * keep.size
        ),
        compiler_params=GRANT,
    )(keep, got)


def merge_send(keep_a, got_a, keep_b, got_b):
    rows, cols = keep_a.shape
    wide = cols // 2

    def body(keep_a, got_a, keep_b, got_b, out_a, out_b):
        out_a[...] = total(keep_a[:, wide:], got_a[:, wide:]).astype(BF16)
        out_b[...] = total(keep_b[:, wide:], got_b[:, wide:]).astype(BF16)

    return pl.pallas_call(
        body,
        in_specs=[VMEM] * 4,
        out_specs=[VMEM] * 2,
        out_shape=[pltpu.VMEM((rows, wide), BF16)] * 2,
        cost_estimate=pl.CostEstimate(
            flops=rows * cols, transcendentals=0, bytes_accessed=6 * rows * cols
        ),
        compiler_params=GRANT,
    )(keep_a, got_a, keep_b, got_b)


def merge_last(table, keep_a, got_a, two_a, keep_b, got_b, two_b):
    rows, cols = keep_a.shape
    n = cols // 4

    def body(table, keep_a, got_a, two_a, keep_b, got_b, two_b, first, last):
        for at, parts in enumerate(((keep_a, got_a, two_a), (keep_b, got_b, two_b))):
            cut = slice(at * rows, (at + 1) * rows)
            for yh in range(2):
                cols = slice(yh * n, (yh + 1) * n)
                value = total(*(part[:, cols] for part in parts))

                @pl.when(table[4] == yh)
                def _():
                    first[cut, :] = value

                @pl.when(table[4] != yh)
                def _():
                    last[cut, :] = value.astype(BF16)

    return pl.pallas_call(
        body,
        in_specs=[SMEM] + [VMEM] * 6,
        out_specs=[VMEM] * 2,
        out_shape=[pltpu.VMEM((2 * rows, n), F32), pltpu.VMEM((2 * rows, n), BF16)],
        cost_estimate=pl.CostEstimate(
            flops=rows * cols, transcendentals=0, bytes_accessed=9 * rows * cols
        ),
        compiler_params=GRANT,
    )(table, keep_a, got_a, two_a, keep_b, got_b, two_b)


def scatter_dp_x(parts, table, scale):
    send_a, keep_a, send_b, keep_b = parts
    got_a = swap(send_a, du=1)
    got_b = swap(send_b, dv=1)
    out_a, out_b = merge_send(keep_a, got_a, keep_b, got_b)
    two_a = swap(out_a, dv=1)
    two_b = swap(out_b, du=1)
    first, last = merge_last(table, keep_a, got_a, two_a, keep_b, got_b, two_b)
    got = swap(last, ds=1)
    return total(first, got) * scale


def scatter_dp_y(parts, scale):
    out, keep = parts
    n = out.shape[1] // 4
    got = swap(out, ds=1)
    send_a, keep_a, send_b, keep_b = cut_sum(keep, got)
    two_a = swap(send_a, du=1)
    two_b = swap(send_b, dv=1)
    out_a = total(keep_a[:, n:], two_a[:, n:]).astype(BF16)
    out_b = total(keep_b[:, n:], two_b[:, n:]).astype(BF16)
    three_a = swap(out_a, dv=1)
    three_b = swap(out_b, du=1)
    own_a = total(keep_a[:, :n], two_a[:, :n], three_a)
    own_b = total(keep_b[:, :n], two_b[:, :n], three_b)
    return jnp.concatenate([own_a, own_b], axis=0) * scale


def contract_cols(left, right):
    return lax.dot_general(left, right, (((1,), (1,)), ((), ())), preferred_element_type=F32)


def forward(scales, pieces, w_gate, w_up):
    n = len(pieces)
    rows = sum(piece.shape[0] for piece in pieces)
    d, ff = w_gate.shape
    wide = min(256, ff)

    def body(scales, w_gate, w_up, *refs):
        ins, (tokens, hidden, to_gate, to_up, sems) = refs[:n], refs[n:]
        for copy in start_copies(ins, tokens, sems):
            copy.wait()
        for at in range(0, ff, wide):
            cols = slice(at, at + wide)
            gate_pre = jnp.dot(tokens[...], w_gate[:, cols], preferred_element_type=F32) * scales[0]
            up_pre = jnp.dot(tokens[...], w_up[:, cols], preferred_element_type=F32) * scales[1]
            sig = jax.nn.sigmoid(gate_pre)
            silu = gate_pre * sig
            hidden[:, cols] = (silu * up_pre).astype(BF16)
            to_up[:, cols] = silu
            to_gate[:, cols] = up_pre * sig * (1.0 + gate_pre * (1.0 - sig))

    return pl.pallas_call(
        body,
        in_specs=[SMEM, VMEM, VMEM] + [HBM] * n,
        out_specs=[VMEM] * 4,
        out_shape=[
            pltpu.VMEM((rows, d), BF16),
            pltpu.VMEM((rows, ff), BF16),
            pltpu.VMEM((rows, ff), F32),
            pltpu.VMEM((rows, ff), F32),
        ],
        scratch_shapes=[pltpu.SemaphoreType.DMA((n,))],
        cost_estimate=pl.CostEstimate(
            flops=4 * rows * d * ff,
            transcendentals=rows * ff,
            bytes_accessed=4 * d * (rows + ff) + 10 * rows * ff,
        ),
        compiler_params=GRANT,
    )(scales, w_gate, w_up, *pieces)


def backward(scales, scaled, w_down, to_gate, to_up):
    rows, d = scaled.shape
    ff = w_down.shape[0]
    tall = rows // 2

    def body(scales, scaled, w_down, to_gate, to_up, d_gate, d_up):
        for at in range(0, rows, tall):
            cut = slice(at, at + tall)
            d_hidden = contract_cols(scaled[cut], w_down[...]) * scales[2]
            d_gate[cut] = (d_hidden * to_gate[cut]).astype(BF16)
            d_up[cut] = (d_hidden * to_up[cut]).astype(BF16)

    return pl.pallas_call(
        body,
        in_specs=[SMEM, VMEM, VMEM, VMEM, VMEM],
        out_specs=[VMEM] * 2,
        out_shape=[pltpu.VMEM((rows, ff), BF16)] * 2,
        cost_estimate=pl.CostEstimate(
            flops=2 * rows * d * ff,
            transcendentals=0,
            bytes_accessed=2 * d * (rows + ff) + 12 * rows * ff,
        ),
        compiler_params=GRANT,
    )(scales, scaled, w_down, to_gate, to_up)


def down(hidden, w_down):
    rows, ff = hidden.shape
    d = w_down.shape[1]
    half, wide = rows // 2, min(1024, d)

    def body(hidden, w_down, other, own):
        @pl.loop(0, d // wide)
        def _(i):
            cols = pl.ds(pl.multiple_of(i * wide, wide), wide)
            value = jnp.dot(hidden[...], w_down[:, cols], preferred_element_type=F32).astype(BF16)
            own[:, cols] = value[:half]
            other[:, cols] = value[half:]

    return pl.pallas_call(
        body,
        in_specs=[VMEM, VMEM],
        out_specs=[VMEM] * 2,
        out_shape=[pltpu.VMEM((half, d), BF16)] * 2,
        cost_estimate=pl.CostEstimate(
            flops=2 * rows * d * ff, transcendentals=0, bytes_accessed=2 * (rows + ff) * (d + ff)
        ),
        compiler_params=GRANT,
    )(hidden, w_down)


def back(scales, d_gate, d_up, w_gate, w_up):
    rows, ff = d_gate.shape
    d = w_gate.shape[0]
    half, wide = rows // 2, min(768, d)

    def body(scales, d_gate, d_up, w_gate, w_up, other, own):
        @pl.loop(0, d // wide)
        def _(i):
            cols = pl.ds(pl.multiple_of(i * wide, wide), wide)
            value = contract_cols(d_gate[...], w_gate[cols, :]) * scales[0]
            value = (value + contract_cols(d_up[...], w_up[cols, :]) * scales[1]).astype(BF16)
            own[:, cols] = value[:half]
            other[:, cols] = value[half:]

    return pl.pallas_call(
        body,
        in_specs=[SMEM] + [VMEM] * 4,
        out_specs=[VMEM] * 2,
        out_shape=[pltpu.VMEM((half, d), BF16)] * 2,
        cost_estimate=pl.CostEstimate(
            flops=4 * rows * d * ff,
            transcendentals=0,
            bytes_accessed=2 * rows * (d + 2 * ff) + 4 * d * ff,
        ),
        compiler_params=GRANT,
    )(scales, d_gate, d_up, w_gate, w_up)


def layer(tokens, expert_ids, route_probs, scale_exps, w_gate, w_up, w_down, out_grad):
    scales = jnp.exp2(scale_exps.astype(F32))
    combine = jnp.sum(jnp.where(expert_ids == 0, route_probs, jnp.zeros_like(route_probs)), axis=1)[
        :, None
    ]
    table = jnp.asarray(place_table())[lax.axis_index("dp")]
    scaled = (combine * out_grad.astype(F32)).astype(BF16)
    w_gate, w_up, w_down = (
        pltpu.with_memory_space_constraint(w, pltpu.VMEM) for w in (w_gate, w_up, w_down)
    )
    token_pieces = gather_blk(tokens)
    scaled_pieces = gather_blk(scaled)
    all_tokens, hidden, to_gate, to_up = forward(scales, token_pieces, w_gate, w_up)
    all_scaled, send_a, keep_a, send_b, keep_b = wgrad_join(table, hidden, scaled_pieces)
    later, combine_later, send_a = lax.optimization_barrier((hidden, combine, send_a))
    grad_down = scatter_dp_x((send_a, keep_a, send_b, keep_b), table, scales[2])

    d_gate, d_up = backward(scales, all_scaled, w_down, to_gate, to_up)
    grad_gate = scatter_dp_y(wgrad_y(table, d_gate, all_tokens), scales[0])
    send_a, keep_a, send_b, keep_b = wgrad_x(table, d_up, all_tokens)
    grad_up = scatter_dp_x((send_a, keep_a, send_b, keep_b), table, scales[1])

    other, own = down(later, w_down)
    expert_out = scatter_blk(own, other) * scales[2]
    mixed = (combine_later * expert_out).astype(BF16)
    other, own = back(scales, d_gate, d_up, w_gate, w_up)
    input_grad = scatter_blk_both(own, other)
    return (
        mixed,
        input_grad.astype(BF16),
        grad_gate.T.astype(BF16),
        grad_up.T.astype(BF16),
        grad_down.astype(BF16),
    )


def solution(mesh):
    return jax.shard_map(
        layer,
        mesh=mesh,
        in_specs=(
            P(("dp", "blk"), None),
            P(("dp", "blk"), None),
            P(("dp", "blk"), None),
            P(),
            P(None, "blk"),
            P(None, "blk"),
            P("blk", None),
            P(("dp", "blk"), None),
        ),
        out_specs=(
            P(("dp", "blk"), None),
            P(("dp", "blk"), None),
            P("dp", "blk"),
            P("dp", "blk"),
            P("blk", "dp"),
        ),
        check_vma=False,
    )
```

```python
import jax
import jax.numpy as jnp
import numpy as np
from jax import lax
from jax.experimental import pallas as pl
from jax.experimental.pallas import tpu as pltpu
from jax.sharding import PartitionSpec as P

BF16 = jnp.bfloat16
F32 = jnp.float32

VMEM = pl.BlockSpec(memory_space=pltpu.VMEM)
SMEM = pl.BlockSpec(memory_space=pltpu.SMEM)
GRANT = pltpu.CompilerParams(vmem_limit_bytes=14 * 2**20)


GRAY = {0: (0, 0), 1: (1, 0), 2: (1, 1), 3: (0, 1)}
UNGRAY = {uv: x for x, uv in GRAY.items()}


def blk_flip(dza, dzb, dyl, dcore):
    pairs = []
    for b in range(16):
        (za, zb), yl, core = GRAY[b // 4], (b // 2) % 2, b % 2
        z = UNGRAY[(za ^ dza, zb ^ dzb)]
        pairs.append((b, z * 4 + (yl ^ dyl) * 2 + (core ^ dcore)))
    return pairs


def dp_flip(du, dv, ds):
    pairs = []
    for d in range(8):
        u, v = GRAY[d // 2]
        pairs.append((d, UNGRAY[(u ^ du, v ^ dv)] * 2 + ((d % 2) ^ ds)))
    return pairs


def place_table():
    rows = np.zeros((8, 5), np.int32)
    for bits in range(4):
        for d, owner in dp_flip(bits >> 1, bits & 1, 0):
            rows[d, bits] = owner // 2
    rows[:, 4] = np.arange(8) % 2
    return rows


def send(value, dza=0, dzb=0, dyl=0, dcore=0):
    return lax.ppermute(value, "blk", blk_flip(dza, dzb, dyl, dcore))


def swap(value, du=0, dv=0, ds=0):
    return lax.ppermute(value, "dp", dp_flip(du, dv, ds))


def gather_blk(mine):
    beside = send(mine, dyl=1)
    a = send(mine, dza=1)
    b = send(mine, dzb=1)
    far = send(mine, dza=1, dzb=1)
    a_beside = send(beside, dza=1)
    b_beside = send(beside, dzb=1)
    far_beside = send(far, dyl=1)
    pieces = [mine, beside, b, b_beside, a, a_beside, far, far_beside]
    return pieces + [send(piece, dcore=1) for piece in pieces]


def total(*parts):
    return sum(part.astype(F32) for part in parts)


def scatter_blk(own, other):
    parts = [own, send(other, dcore=1)]
    for flip in ({"dza": 1}, {"dzb": 1}, {"dyl": 1}):
        half = parts[0].shape[0] // 2
        out = total(*(part[half:] for part in parts)).astype(BF16)
        parts = [part[:half] for part in parts] + [send(out, **flip)]
    return total(*parts)


def merge_rows(own, got):
    rows, d = own.shape
    n = rows // 8

    def body(own, got, near, far_a, far_b):
        near[...] = total(own[: 6 * n], got[: 6 * n]).astype(BF16)
        far_a[...] = total(own[6 * n : 7 * n], got[6 * n : 7 * n]).astype(BF16)
        far_b[...] = total(own[7 * n :], got[7 * n :]).astype(BF16)

    return pl.pallas_call(
        body,
        in_specs=[VMEM] * 2,
        out_specs=[VMEM] * 3,
        out_shape=[pltpu.VMEM((count * n, d), BF16) for count in (6, 1, 1)],
        cost_estimate=pl.CostEstimate(
            flops=rows * d, transcendentals=0, bytes_accessed=6 * rows * d
        ),
        compiler_params=GRANT,
    )(own, got)


def scatter_blk_both(own, other):
    got = send(other, dcore=1)
    n = own.shape[0] // 8
    near, far_a, far_b = merge_rows(own, got)
    rows = [near[i * n : (i + 1) * n] for i in range(6)]
    from_a = send(far_a, dza=1)
    from_b = send(far_b, dzb=1)
    b = jnp.concatenate([total(rows[2], from_a), total(rows[3])], axis=0).astype(BF16)
    a = jnp.concatenate([total(rows[4]), total(rows[5], from_b)], axis=0).astype(BF16)
    got_b = send(b, dzb=1)
    got_a = send(a, dza=1)
    out = total(rows[1], got_b[n:], got_a[n:]).astype(BF16)
    last = send(out, dyl=1)
    return total(rows[0], got_b[:n], got_a[:n], last)


def join(pieces, target):
    at = 0
    for piece in pieces:
        target[at : at + piece.shape[0]] = piece[...]
        at += piece.shape[0]


def load(*arrays):
    n = len(arrays)

    def body(*refs):
        for i in range(n):
            tall = arrays[i].shape[0] // 8

            @pl.loop(0, 8)
            def _(j):
                cut = pl.ds(pl.multiple_of(j * tall, tall), tall)
                refs[n + i][cut, :] = refs[i][cut, :]

    return pl.pallas_call(
        body,
        in_specs=[VMEM] * n,
        out_specs=[VMEM] * n,
        out_shape=[pltpu.VMEM(array.shape, array.dtype) for array in arrays],
        cost_estimate=pl.CostEstimate(
            flops=0, transcendentals=0, bytes_accessed=2 * sum(array.size for array in arrays)
        ),
        compiler_params=GRANT,
    )(*arrays)


def wgrad_cost(rows, ff, d):
    return pl.CostEstimate(
        flops=2 * rows * ff * d, transcendentals=0, bytes_accessed=2 * (rows * (ff + d) + ff * d)
    )


def wgrad_join(table, left, pieces):
    rows, ff = left.shape
    d = pieces[0].shape[1]
    n = len(pieces)

    def body(table, left, *refs):
        ins, (right, *outs), left_t = refs[:n], refs[n : n + 5], refs[n + 5]
        join(ins, right)
        left_t[...] = left[...].T
        cut_x(table, left_t, right, *outs)

    part = pltpu.VMEM((ff // 2, d // 2), BF16)
    return pl.pallas_call(
        body,
        in_specs=[SMEM, VMEM] + [VMEM] * n,
        out_specs=[VMEM] * 5,
        out_shape=[pltpu.VMEM((rows, d), BF16)] + [part] * 4,
        scratch_shapes=[pltpu.VMEM((ff, rows), BF16)],
        cost_estimate=wgrad_cost(rows, ff, d),
        compiler_params=GRANT,
    )(table, left, *pieces)


def chunk(right, table, j, wide):
    return right[:, pl.ds(pl.multiple_of(table[j] * wide, wide), wide)]


def cut_x(table, left_t, right, send_a, keep_a, send_b, keep_b):
    half, wide = left_t.shape[0] // 2, right.shape[1] // 4
    for j in range(4):
        u, v = j >> 1, j & 1
        value = jnp.dot(
            left_t[...], chunk(right, table, j, wide), preferred_element_type=F32
        ).astype(BF16)
        to_a = send_a if u else keep_a
        to_b = send_b if v else keep_b
        to_a[:, v * wide : (v + 1) * wide] = value[:half]
        to_b[:, u * wide : (u + 1) * wide] = value[half:]


def wgrad_x(table, left, right):
    rows, ff = left.shape
    d = right.shape[1]

    def body(table, left, right, send_a, keep_a, send_b, keep_b, left_t):
        left_t[...] = left[...].T
        cut_x(table, left_t, right, send_a, keep_a, send_b, keep_b)

    return pl.pallas_call(
        body,
        in_specs=[SMEM, VMEM, VMEM],
        out_specs=[VMEM] * 4,
        out_shape=[pltpu.VMEM((ff // 2, d // 2), BF16)] * 4,
        scratch_shapes=[pltpu.VMEM((ff, rows), BF16)],
        cost_estimate=wgrad_cost(rows, ff, d),
        compiler_params=GRANT,
    )(table, left, right)


def wgrad_y(table, left, right):
    rows, ff = left.shape
    d = right.shape[1]
    wide = d // 4
    n = wide // 2

    def body(table, left, right, out, keep, left_t):
        left_t[...] = left[...].T
        for j in range(4):
            cols = slice(j * n, (j + 1) * n)
            value = jnp.dot(
                left_t[...], chunk(right, table, j, wide), preferred_element_type=F32
            ).astype(BF16)

            @pl.when(table[4] == 0)
            def _():
                keep[:, cols] = value[:, :n]
                out[:, cols] = value[:, n:]

            @pl.when(table[4] != 0)
            def _():
                out[:, cols] = value[:, :n]
                keep[:, cols] = value[:, n:]

    return pl.pallas_call(
        body,
        in_specs=[SMEM, VMEM, VMEM],
        out_specs=[VMEM] * 2,
        out_shape=[pltpu.VMEM((ff, d // 2), BF16)] * 2,
        scratch_shapes=[pltpu.VMEM((ff, rows), BF16)],
        cost_estimate=wgrad_cost(rows, ff, d),
        compiler_params=GRANT,
    )(table, left, right)


def cut_sum(keep, got):
    half, n = keep.shape[0] // 2, keep.shape[1] // 4

    def body(keep, got, send_a, keep_a, send_b, keep_b):
        for j in range(4):
            u, v = j >> 1, j & 1
            cols = slice(j * n, (j + 1) * n)
            value = total(keep[:, cols], got[:, cols]).astype(BF16)
            to_a = send_a if u else keep_a
            to_b = send_b if v else keep_b
            to_a[:, v * n : (v + 1) * n] = value[:half]
            to_b[:, u * n : (u + 1) * n] = value[half:]

    return pl.pallas_call(
        body,
        in_specs=[VMEM] * 2,
        out_specs=[VMEM] * 4,
        out_shape=[pltpu.VMEM((half, 2 * n), BF16)] * 4,
        cost_estimate=pl.CostEstimate(
            flops=keep.size, transcendentals=0, bytes_accessed=6 * keep.size
        ),
        compiler_params=GRANT,
    )(keep, got)


def merge_send(keep_a, got_a, keep_b, got_b):
    rows, cols = keep_a.shape
    wide = cols // 2

    def body(keep_a, got_a, keep_b, got_b, out_a, out_b):
        out_a[...] = total(keep_a[:, wide:], got_a[:, wide:]).astype(BF16)
        out_b[...] = total(keep_b[:, wide:], got_b[:, wide:]).astype(BF16)

    return pl.pallas_call(
        body,
        in_specs=[VMEM] * 4,
        out_specs=[VMEM] * 2,
        out_shape=[pltpu.VMEM((rows, wide), BF16)] * 2,
        cost_estimate=pl.CostEstimate(
            flops=rows * cols, transcendentals=0, bytes_accessed=6 * rows * cols
        ),
        compiler_params=GRANT,
    )(keep_a, got_a, keep_b, got_b)


def merge_last(table, keep_a, got_a, two_a, keep_b, got_b, two_b):
    rows, cols = keep_a.shape
    n = cols // 4

    def body(table, keep_a, got_a, two_a, keep_b, got_b, two_b, first, last):
        for at, parts in enumerate(((keep_a, got_a, two_a), (keep_b, got_b, two_b))):
            cut = slice(at * rows, (at + 1) * rows)
            for yh in range(2):
                cols = slice(yh * n, (yh + 1) * n)
                value = total(*(part[:, cols] for part in parts))

                @pl.when(table[4] == yh)
                def _():
                    first[cut, :] = value

                @pl.when(table[4] != yh)
                def _():
                    last[cut, :] = value.astype(BF16)

    return pl.pallas_call(
        body,
        in_specs=[SMEM] + [VMEM] * 6,
        out_specs=[VMEM] * 2,
        out_shape=[pltpu.VMEM((2 * rows, n), F32), pltpu.VMEM((2 * rows, n), BF16)],
        cost_estimate=pl.CostEstimate(
            flops=rows * cols, transcendentals=0, bytes_accessed=9 * rows * cols
        ),
        compiler_params=GRANT,
    )(table, keep_a, got_a, two_a, keep_b, got_b, two_b)


def finish(scales, k, parts, flip):
    n = parts[0][-1].shape[1]
    rows = sum(block[-1].shape[0] for block in parts)
    flat = [part for block in parts for part in block]

    def body(scales, *refs):
        refs, out = list(refs[:-1]), refs[-1]
        at = 0
        for block in parts:
            some = [refs.pop(0)[:, :n] for _ in block]
            value = (total(*some) * scales[k]).astype(BF16)
            cut = slice(at, at + value.shape[0])
            if flip:
                out[:, cut] = value.T
            else:
                out[cut, :] = value
            at += value.shape[0]

    return pl.pallas_call(
        body,
        in_specs=[SMEM] + [VMEM] * len(flat),
        out_specs=VMEM,
        out_shape=jax.ShapeDtypeStruct((n, rows) if flip else (rows, n), BF16),
        cost_estimate=pl.CostEstimate(
            flops=3 * rows * n, transcendentals=0, bytes_accessed=8 * rows * n
        ),
        compiler_params=GRANT,
    )(scales, *flat)


def scatter_dp_x(parts, table, scales, k, flip):
    send_a, keep_a, send_b, keep_b = parts
    got_a = swap(send_a, du=1)
    got_b = swap(send_b, dv=1)
    out_a, out_b = merge_send(keep_a, got_a, keep_b, got_b)
    two_a = swap(out_a, dv=1)
    two_b = swap(out_b, du=1)
    first, last = merge_last(table, keep_a, got_a, two_a, keep_b, got_b, two_b)
    got = swap(last, ds=1)
    return finish(scales, k, [[first, got]], flip)


def scatter_dp_y(parts, scales, k, flip):
    out, keep = parts
    n = out.shape[1] // 4
    got = swap(out, ds=1)
    send_a, keep_a, send_b, keep_b = cut_sum(keep, got)
    two_a = swap(send_a, du=1)
    two_b = swap(send_b, dv=1)
    out_a = total(keep_a[:, n:], two_a[:, n:]).astype(BF16)
    out_b = total(keep_b[:, n:], two_b[:, n:]).astype(BF16)
    three_a = swap(out_a, dv=1)
    three_b = swap(out_b, du=1)
    return finish(scales, k, [[keep_a, two_a, three_a], [keep_b, two_b, three_b]], flip)


def contract_cols(left, right):
    return lax.dot_general(left, right, (((1,), (1,)), ((), ())), preferred_element_type=F32)


def forward(scales, pieces, w_gate, w_up):
    n = len(pieces)
    rows = sum(piece.shape[0] for piece in pieces)
    d, ff = w_gate.shape
    wide = min(256, ff)

    def body(scales, w_gate, w_up, *refs):
        ins, (tokens, hidden, to_gate, to_up) = refs[:n], refs[n:]
        join(ins, tokens)
        for at in range(0, ff, wide):
            cols = slice(at, at + wide)
            gate_pre = jnp.dot(tokens[...], w_gate[:, cols], preferred_element_type=F32) * scales[0]
            up_pre = jnp.dot(tokens[...], w_up[:, cols], preferred_element_type=F32) * scales[1]
            sig = jax.nn.sigmoid(gate_pre)
            silu = gate_pre * sig
            hidden[:, cols] = (silu * up_pre).astype(BF16)
            to_up[:, cols] = silu
            to_gate[:, cols] = up_pre * sig * (1.0 + gate_pre * (1.0 - sig))

    return pl.pallas_call(
        body,
        in_specs=[SMEM, VMEM, VMEM] + [VMEM] * n,
        out_specs=[VMEM] * 4,
        out_shape=[
            pltpu.VMEM((rows, d), BF16),
            pltpu.VMEM((rows, ff), BF16),
            pltpu.VMEM((rows, ff), F32),
            pltpu.VMEM((rows, ff), F32),
        ],
        cost_estimate=pl.CostEstimate(
            flops=4 * rows * d * ff,
            transcendentals=rows * ff,
            bytes_accessed=4 * d * (rows + ff) + 10 * rows * ff,
        ),
        compiler_params=GRANT,
    )(scales, w_gate, w_up, *pieces)


def backward(scales, scaled, w_down, to_gate, to_up):
    rows, d = scaled.shape
    ff = w_down.shape[0]
    tall = rows // 2

    def body(scales, scaled, w_down, to_gate, to_up, d_gate, d_up):
        for at in range(0, rows, tall):
            cut = slice(at, at + tall)
            d_hidden = contract_cols(scaled[cut], w_down[...]) * scales[2]
            d_gate[cut] = (d_hidden * to_gate[cut]).astype(BF16)
            d_up[cut] = (d_hidden * to_up[cut]).astype(BF16)

    return pl.pallas_call(
        body,
        in_specs=[SMEM, VMEM, VMEM, VMEM, VMEM],
        out_specs=[VMEM] * 2,
        out_shape=[pltpu.VMEM((rows, ff), BF16)] * 2,
        cost_estimate=pl.CostEstimate(
            flops=2 * rows * d * ff,
            transcendentals=0,
            bytes_accessed=2 * d * (rows + ff) + 12 * rows * ff,
        ),
        compiler_params=GRANT,
    )(scales, scaled, w_down, to_gate, to_up)


def down(hidden, w_down):
    rows, ff = hidden.shape
    d = w_down.shape[1]
    half, wide = rows // 2, min(1024, d)

    def body(hidden, w_down, other, own):
        @pl.loop(0, d // wide)
        def _(i):
            cols = pl.ds(pl.multiple_of(i * wide, wide), wide)
            value = jnp.dot(hidden[...], w_down[:, cols], preferred_element_type=F32).astype(BF16)
            own[:, cols] = value[:half]
            other[:, cols] = value[half:]

    return pl.pallas_call(
        body,
        in_specs=[VMEM, VMEM],
        out_specs=[VMEM] * 2,
        out_shape=[pltpu.VMEM((half, d), BF16)] * 2,
        cost_estimate=pl.CostEstimate(
            flops=2 * rows * d * ff, transcendentals=0, bytes_accessed=2 * (rows + ff) * (d + ff)
        ),
        compiler_params=GRANT,
    )(hidden, w_down)


def back(scales, d_gate, d_up, w_gate, w_up):
    rows, ff = d_gate.shape
    d = w_gate.shape[0]
    half, wide = rows // 2, min(768, d)

    def body(scales, d_gate, d_up, w_gate, w_up, other, own):
        @pl.loop(0, d // wide)
        def _(i):
            cols = pl.ds(pl.multiple_of(i * wide, wide), wide)
            value = contract_cols(d_gate[...], w_gate[cols, :]) * scales[0]
            value = (value + contract_cols(d_up[...], w_up[cols, :]) * scales[1]).astype(BF16)
            own[:, cols] = value[:half]
            other[:, cols] = value[half:]

    return pl.pallas_call(
        body,
        in_specs=[SMEM] + [VMEM] * 4,
        out_specs=[VMEM] * 2,
        out_shape=[pltpu.VMEM((half, d), BF16)] * 2,
        cost_estimate=pl.CostEstimate(
            flops=4 * rows * d * ff,
            transcendentals=0,
            bytes_accessed=2 * rows * (d + 2 * ff) + 4 * d * ff,
        ),
        compiler_params=GRANT,
    )(scales, d_gate, d_up, w_gate, w_up)


def layer(tokens, expert_ids, route_probs, scale_exps, w_gate, w_up, w_down, out_grad):
    scales = jnp.exp2(scale_exps.astype(F32))
    combine = jnp.sum(jnp.where(expert_ids == 0, route_probs, jnp.zeros_like(route_probs)), axis=1)[
        :, None
    ]
    table = jnp.asarray(place_table())[lax.axis_index("dp")]
    scaled = (combine * out_grad.astype(F32)).astype(BF16)
    w_gate_now, w_up_now = load(w_gate)[0], load(w_up)[0]
    w_gate, w_up, w_down = (
        pltpu.with_memory_space_constraint(w, pltpu.VMEM) for w in (w_gate, w_up, w_down)
    )
    token_pieces = gather_blk(tokens)
    scaled_pieces = gather_blk(scaled)
    all_tokens, hidden, to_gate, to_up = forward(scales, token_pieces, w_gate_now, w_up_now)
    all_scaled, send_a, keep_a, send_b, keep_b = wgrad_join(table, hidden, scaled_pieces)
    later, combine_later, send_a = lax.optimization_barrier((hidden, combine, send_a))
    grad_down = scatter_dp_x((send_a, keep_a, send_b, keep_b), table, scales, 2, False)

    d_gate, d_up = backward(scales, all_scaled, w_down, to_gate, to_up)
    grad_gate = scatter_dp_y(wgrad_y(table, d_gate, all_tokens), scales, 0, True)
    send_a, keep_a, send_b, keep_b = wgrad_x(table, d_up, all_tokens)
    grad_up = scatter_dp_x((send_a, keep_a, send_b, keep_b), table, scales, 1, True)

    other, own = down(later, w_down)
    expert_out = scatter_blk(own, other) * scales[2]
    mixed = (combine_later * expert_out).astype(BF16)
    other, own = back(scales, d_gate, d_up, w_gate, w_up)
    input_grad = scatter_blk_both(own, other)
    return (
        mixed,
        input_grad.astype(BF16),
        grad_gate,
        grad_up,
        grad_down,
    )


def solution(mesh):
    return jax.shard_map(
        layer,
        mesh=mesh,
        in_specs=(
            P(("dp", "blk"), None),
            P(("dp", "blk"), None),
            P(("dp", "blk"), None),
            P(),
            P(None, "blk"),
            P(None, "blk"),
            P("blk", None),
            P(("dp", "blk"), None),
        ),
        out_specs=(
            P(("dp", "blk"), None),
            P(("dp", "blk"), None),
            P("dp", "blk"),
            P("dp", "blk"),
            P("blk", "dp"),
        ),
        check_vma=False,
    )
```

```python
import jax
import jax.numpy as jnp
import numpy as np
from jax import lax
from jax.experimental import pallas as pl
from jax.experimental.pallas import tpu as pltpu
from jax.sharding import PartitionSpec as P

BF16 = jnp.bfloat16
F32 = jnp.float32

VMEM = pl.BlockSpec(memory_space=pltpu.VMEM)
SMEM = pl.BlockSpec(memory_space=pltpu.SMEM)
GRANT = pltpu.CompilerParams(vmem_limit_bytes=14 * 2**20)


GRAY = {0: (0, 0), 1: (1, 0), 2: (1, 1), 3: (0, 1)}
UNGRAY = {uv: x for x, uv in GRAY.items()}


def blk_flip(dza, dzb, dyl, dcore):
    pairs = []
    for b in range(16):
        (za, zb), yl, core = GRAY[b // 4], (b // 2) % 2, b % 2
        z = UNGRAY[(za ^ dza, zb ^ dzb)]
        pairs.append((b, z * 4 + (yl ^ dyl) * 2 + (core ^ dcore)))
    return pairs


def dp_flip(du, dv, ds):
    pairs = []
    for d in range(8):
        u, v = GRAY[d // 2]
        pairs.append((d, UNGRAY[(u ^ du, v ^ dv)] * 2 + ((d % 2) ^ ds)))
    return pairs


def place_table():
    rows = np.zeros((8, 5), np.int32)
    for bits in range(4):
        for d, owner in dp_flip(bits >> 1, bits & 1, 0):
            rows[d, bits] = owner // 2
    rows[:, 4] = np.arange(8) % 2
    return rows


def send(value, dza=0, dzb=0, dyl=0, dcore=0):
    return lax.ppermute(value, "blk", blk_flip(dza, dzb, dyl, dcore))


def swap(value, du=0, dv=0, ds=0):
    return lax.ppermute(value, "dp", dp_flip(du, dv, ds))


def gather_blk(mine):
    beside = send(mine, dyl=1)
    a = send(mine, dza=1)
    b = send(mine, dzb=1)
    far = send(mine, dza=1, dzb=1)
    a_beside = send(beside, dza=1)
    b_beside = send(beside, dzb=1)
    far_beside = send(far, dyl=1)
    pieces = [mine, beside, b, b_beside, a, a_beside, far, far_beside]
    return pieces + [send(piece, dcore=1) for piece in pieces]


def total(*parts):
    return sum(part.astype(F32) for part in parts)


def merge_rows(own, got):
    rows, d = own.shape
    n = rows // 8

    def body(own, got, near, far_a, far_b):
        near[...] = total(own[: 6 * n], got[: 6 * n]).astype(BF16)
        far_a[...] = total(own[6 * n : 7 * n], got[6 * n : 7 * n]).astype(BF16)
        far_b[...] = total(own[7 * n :], got[7 * n :]).astype(BF16)

    return pl.pallas_call(
        body,
        in_specs=[VMEM] * 2,
        out_specs=[VMEM] * 3,
        out_shape=[pltpu.VMEM((count * n, d), BF16) for count in (6, 1, 1)],
        cost_estimate=pl.CostEstimate(
            flops=rows * d, transcendentals=0, bytes_accessed=6 * rows * d
        ),
        compiler_params=GRANT,
    )(own, got)


def scatter_blk(own, other):
    got = send(other, dcore=1)
    n = own.shape[0] // 8
    near, far_a, far_b = merge_rows(own, got)
    rows = [near[i * n : (i + 1) * n] for i in range(6)]
    from_a = send(far_a, dza=1)
    from_b = send(far_b, dzb=1)
    b = jnp.concatenate([total(rows[2], from_a), total(rows[3])], axis=0).astype(BF16)
    a = jnp.concatenate([total(rows[4]), total(rows[5], from_b)], axis=0).astype(BF16)
    got_b = send(b, dzb=1)
    got_a = send(a, dza=1)
    out = total(rows[1], got_b[n:], got_a[n:]).astype(BF16)
    last = send(out, dyl=1)
    return total(rows[0], got_b[:n], got_a[:n], last)


def join(pieces, target):
    at = 0
    for piece in pieces:
        target[at : at + piece.shape[0]] = piece[...]
        at += piece.shape[0]


def load(*arrays):
    n = len(arrays)

    def body(*refs):
        for i in range(n):
            tall = arrays[i].shape[0] // 8

            @pl.loop(0, 8)
            def _(j):
                cut = pl.ds(pl.multiple_of(j * tall, tall), tall)
                refs[n + i][cut, :] = refs[i][cut, :]

    return pl.pallas_call(
        body,
        in_specs=[VMEM] * n,
        out_specs=[VMEM] * n,
        out_shape=[pltpu.VMEM(array.shape, array.dtype) for array in arrays],
        cost_estimate=pl.CostEstimate(
            flops=0, transcendentals=0, bytes_accessed=2 * sum(array.size for array in arrays)
        ),
        compiler_params=GRANT,
    )(*arrays)


def wgrad_cost(rows, ff, d):
    return pl.CostEstimate(
        flops=2 * rows * ff * d, transcendentals=0, bytes_accessed=2 * (rows * (ff + d) + ff * d)
    )


def wgrad_join(table, left, pieces):
    rows, ff = left.shape
    d = pieces[0].shape[1]
    n = len(pieces)

    def body(table, left, *refs):
        ins, (right, *outs), left_t = refs[:n], refs[n : n + 5], refs[n + 5]
        join(ins, right)
        left_t[...] = left[...].T
        cut_x(table, left_t, right, *outs)

    part = pltpu.VMEM((ff // 2, d // 2), BF16)
    return pl.pallas_call(
        body,
        in_specs=[SMEM, VMEM] + [VMEM] * n,
        out_specs=[VMEM] * 5,
        out_shape=[pltpu.VMEM((rows, d), BF16)] + [part] * 4,
        scratch_shapes=[pltpu.VMEM((ff, rows), BF16)],
        cost_estimate=wgrad_cost(rows, ff, d),
        compiler_params=GRANT,
    )(table, left, *pieces)


def chunk(right, table, j, wide):
    return right[:, pl.ds(pl.multiple_of(table[j] * wide, wide), wide)]


def cut_x(table, left_t, right, send_a, keep_a, send_b, keep_b):
    half, wide = left_t.shape[0] // 2, right.shape[1] // 4
    for j in range(4):
        u, v = j >> 1, j & 1
        value = jnp.dot(
            left_t[...], chunk(right, table, j, wide), preferred_element_type=F32
        ).astype(BF16)
        to_a = send_a if u else keep_a
        to_b = send_b if v else keep_b
        to_a[:, v * wide : (v + 1) * wide] = value[:half]
        to_b[:, u * wide : (u + 1) * wide] = value[half:]


def wgrad_x(table, left, right):
    rows, ff = left.shape
    d = right.shape[1]

    def body(table, left, right, send_a, keep_a, send_b, keep_b, left_t):
        left_t[...] = left[...].T
        cut_x(table, left_t, right, send_a, keep_a, send_b, keep_b)

    return pl.pallas_call(
        body,
        in_specs=[SMEM, VMEM, VMEM],
        out_specs=[VMEM] * 4,
        out_shape=[pltpu.VMEM((ff // 2, d // 2), BF16)] * 4,
        scratch_shapes=[pltpu.VMEM((ff, rows), BF16)],
        cost_estimate=wgrad_cost(rows, ff, d),
        compiler_params=GRANT,
    )(table, left, right)


def wgrad_y(table, left, right):
    rows, ff = left.shape
    d = right.shape[1]
    wide = d // 4
    n = wide // 2

    def body(table, left, right, out, keep, left_t):
        left_t[...] = left[...].T
        for j in range(4):
            cols = slice(j * n, (j + 1) * n)
            value = jnp.dot(
                left_t[...], chunk(right, table, j, wide), preferred_element_type=F32
            ).astype(BF16)

            @pl.when(table[4] == 0)
            def _():
                keep[:, cols] = value[:, :n]
                out[:, cols] = value[:, n:]

            @pl.when(table[4] != 0)
            def _():
                out[:, cols] = value[:, :n]
                keep[:, cols] = value[:, n:]

    return pl.pallas_call(
        body,
        in_specs=[SMEM, VMEM, VMEM],
        out_specs=[VMEM] * 2,
        out_shape=[pltpu.VMEM((ff, d // 2), BF16)] * 2,
        scratch_shapes=[pltpu.VMEM((ff, rows), BF16)],
        cost_estimate=wgrad_cost(rows, ff, d),
        compiler_params=GRANT,
    )(table, left, right)


def cut_sum(keep, got):
    half, n = keep.shape[0] // 2, keep.shape[1] // 4

    def body(keep, got, send_a, keep_a, send_b, keep_b):
        for j in range(4):
            u, v = j >> 1, j & 1
            cols = slice(j * n, (j + 1) * n)
            value = total(keep[:, cols], got[:, cols]).astype(BF16)
            to_a = send_a if u else keep_a
            to_b = send_b if v else keep_b
            to_a[:, v * n : (v + 1) * n] = value[:half]
            to_b[:, u * n : (u + 1) * n] = value[half:]

    return pl.pallas_call(
        body,
        in_specs=[VMEM] * 2,
        out_specs=[VMEM] * 4,
        out_shape=[pltpu.VMEM((half, 2 * n), BF16)] * 4,
        cost_estimate=pl.CostEstimate(
            flops=keep.size, transcendentals=0, bytes_accessed=6 * keep.size
        ),
        compiler_params=GRANT,
    )(keep, got)


def merge_send(keep_a, got_a, keep_b, got_b):
    rows, cols = keep_a.shape
    wide = cols // 2

    def body(keep_a, got_a, keep_b, got_b, out_a, out_b):
        out_a[...] = total(keep_a[:, wide:], got_a[:, wide:]).astype(BF16)
        out_b[...] = total(keep_b[:, wide:], got_b[:, wide:]).astype(BF16)

    return pl.pallas_call(
        body,
        in_specs=[VMEM] * 4,
        out_specs=[VMEM] * 2,
        out_shape=[pltpu.VMEM((rows, wide), BF16)] * 2,
        cost_estimate=pl.CostEstimate(
            flops=rows * cols, transcendentals=0, bytes_accessed=6 * rows * cols
        ),
        compiler_params=GRANT,
    )(keep_a, got_a, keep_b, got_b)


def merge_last(table, keep_a, got_a, two_a, keep_b, got_b, two_b):
    rows, cols = keep_a.shape
    n = cols // 4

    def body(table, keep_a, got_a, two_a, keep_b, got_b, two_b, first, last):
        for at, parts in enumerate(((keep_a, got_a, two_a), (keep_b, got_b, two_b))):
            cut = slice(at * rows, (at + 1) * rows)
            for yh in range(2):
                cols = slice(yh * n, (yh + 1) * n)
                value = total(*(part[:, cols] for part in parts))

                @pl.when(table[4] == yh)
                def _():
                    first[cut, :] = value

                @pl.when(table[4] != yh)
                def _():
                    last[cut, :] = value.astype(BF16)

    return pl.pallas_call(
        body,
        in_specs=[SMEM] + [VMEM] * 6,
        out_specs=[VMEM] * 2,
        out_shape=[pltpu.VMEM((2 * rows, n), F32), pltpu.VMEM((2 * rows, n), BF16)],
        cost_estimate=pl.CostEstimate(
            flops=rows * cols, transcendentals=0, bytes_accessed=9 * rows * cols
        ),
        compiler_params=GRANT,
    )(table, keep_a, got_a, two_a, keep_b, got_b, two_b)


def finish(scales, k, parts, flip):
    n = parts[0][-1].shape[1]
    rows = sum(block[-1].shape[0] for block in parts)
    flat = [part for block in parts for part in block]

    def body(scales, *refs):
        refs, out = list(refs[:-1]), refs[-1]
        at = 0
        for block in parts:
            some = [refs.pop(0)[:, :n] for _ in block]
            value = (total(*some) * scales[k]).astype(BF16)
            cut = slice(at, at + value.shape[0])
            if flip:
                out[:, cut] = value.T
            else:
                out[cut, :] = value
            at += value.shape[0]

    return pl.pallas_call(
        body,
        in_specs=[SMEM] + [VMEM] * len(flat),
        out_specs=VMEM,
        out_shape=jax.ShapeDtypeStruct((n, rows) if flip else (rows, n), BF16),
        cost_estimate=pl.CostEstimate(
            flops=3 * rows * n, transcendentals=0, bytes_accessed=8 * rows * n
        ),
        compiler_params=GRANT,
    )(scales, *flat)


def scatter_dp_x(parts, table, scales, k, flip):
    send_a, keep_a, send_b, keep_b = parts
    got_a = swap(send_a, du=1)
    got_b = swap(send_b, dv=1)
    out_a, out_b = merge_send(keep_a, got_a, keep_b, got_b)
    two_a = swap(out_a, dv=1)
    two_b = swap(out_b, du=1)
    first, last = merge_last(table, keep_a, got_a, two_a, keep_b, got_b, two_b)
    got = swap(last, ds=1)
    return finish(scales, k, [[first, got]], flip)


def scatter_dp_y(parts, scales, k, flip):
    out, keep = parts
    n = out.shape[1] // 4
    got = swap(out, ds=1)
    send_a, keep_a, send_b, keep_b = cut_sum(keep, got)
    two_a = swap(send_a, du=1)
    two_b = swap(send_b, dv=1)
    out_a = total(keep_a[:, n:], two_a[:, n:]).astype(BF16)
    out_b = total(keep_b[:, n:], two_b[:, n:]).astype(BF16)
    three_a = swap(out_a, dv=1)
    three_b = swap(out_b, du=1)
    return finish(scales, k, [[keep_a, two_a, three_a], [keep_b, two_b, three_b]], flip)


def contract_cols(left, right):
    return lax.dot_general(left, right, (((1,), (1,)), ((), ())), preferred_element_type=F32)


def forward(scales, pieces, w_gate, w_up):
    n = len(pieces)
    rows = sum(piece.shape[0] for piece in pieces)
    d, ff = w_gate.shape
    wide = min(256, ff)

    def body(scales, w_gate, w_up, *refs):
        ins, (tokens, hidden, to_gate, to_up) = refs[:n], refs[n:]
        join(ins, tokens)
        for at in range(0, ff, wide):
            cols = slice(at, at + wide)
            gate_pre = jnp.dot(tokens[...], w_gate[:, cols], preferred_element_type=F32) * scales[0]
            up_pre = jnp.dot(tokens[...], w_up[:, cols], preferred_element_type=F32) * scales[1]
            sig = jax.nn.sigmoid(gate_pre)
            silu = gate_pre * sig
            hidden[:, cols] = (silu * up_pre).astype(BF16)
            to_up[:, cols] = silu
            to_gate[:, cols] = up_pre * sig * (1.0 + gate_pre * (1.0 - sig))

    return pl.pallas_call(
        body,
        in_specs=[SMEM, VMEM, VMEM] + [VMEM] * n,
        out_specs=[VMEM] * 4,
        out_shape=[
            pltpu.VMEM((rows, d), BF16),
            pltpu.VMEM((rows, ff), BF16),
            pltpu.VMEM((rows, ff), F32),
            pltpu.VMEM((rows, ff), F32),
        ],
        cost_estimate=pl.CostEstimate(
            flops=4 * rows * d * ff,
            transcendentals=rows * ff,
            bytes_accessed=4 * d * (rows + ff) + 10 * rows * ff,
        ),
        compiler_params=GRANT,
    )(scales, w_gate, w_up, *pieces)


def backward(scales, scaled, w_down, to_gate, to_up):
    rows, d = scaled.shape
    ff = w_down.shape[0]
    tall = rows // 2

    def body(scales, scaled, w_down, to_gate, to_up, d_gate, d_up):
        for at in range(0, rows, tall):
            cut = slice(at, at + tall)
            d_hidden = contract_cols(scaled[cut], w_down[...]) * scales[2]
            d_gate[cut] = (d_hidden * to_gate[cut]).astype(BF16)
            d_up[cut] = (d_hidden * to_up[cut]).astype(BF16)

    return pl.pallas_call(
        body,
        in_specs=[SMEM, VMEM, VMEM, VMEM, VMEM],
        out_specs=[VMEM] * 2,
        out_shape=[pltpu.VMEM((rows, ff), BF16)] * 2,
        cost_estimate=pl.CostEstimate(
            flops=2 * rows * d * ff,
            transcendentals=0,
            bytes_accessed=2 * d * (rows + ff) + 12 * rows * ff,
        ),
        compiler_params=GRANT,
    )(scales, scaled, w_down, to_gate, to_up)


def down(hidden, w_down):
    rows, ff = hidden.shape
    d = w_down.shape[1]
    half, wide = rows // 2, min(1024, d)

    def body(hidden, w_down, other, own):
        @pl.loop(0, d // wide)
        def _(i):
            cols = pl.ds(pl.multiple_of(i * wide, wide), wide)
            value = jnp.dot(hidden[...], w_down[:, cols], preferred_element_type=F32).astype(BF16)
            own[:, cols] = value[:half]
            other[:, cols] = value[half:]

    return pl.pallas_call(
        body,
        in_specs=[VMEM, VMEM],
        out_specs=[VMEM] * 2,
        out_shape=[pltpu.VMEM((half, d), BF16)] * 2,
        cost_estimate=pl.CostEstimate(
            flops=2 * rows * d * ff, transcendentals=0, bytes_accessed=2 * (rows + ff) * (d + ff)
        ),
        compiler_params=GRANT,
    )(hidden, w_down)


def back(scales, d_gate, d_up, w_gate, w_up):
    rows, ff = d_gate.shape
    d = w_gate.shape[0]
    half, wide = rows // 2, min(768, d)

    def body(scales, d_gate, d_up, w_gate, w_up, other, own):
        @pl.loop(0, d // wide)
        def _(i):
            cols = pl.ds(pl.multiple_of(i * wide, wide), wide)
            value = contract_cols(d_gate[...], w_gate[cols, :]) * scales[0]
            value = (value + contract_cols(d_up[...], w_up[cols, :]) * scales[1]).astype(BF16)
            own[:, cols] = value[:half]
            other[:, cols] = value[half:]

    return pl.pallas_call(
        body,
        in_specs=[SMEM] + [VMEM] * 4,
        out_specs=[VMEM] * 2,
        out_shape=[pltpu.VMEM((half, d), BF16)] * 2,
        cost_estimate=pl.CostEstimate(
            flops=4 * rows * d * ff,
            transcendentals=0,
            bytes_accessed=2 * rows * (d + 2 * ff) + 4 * d * ff,
        ),
        compiler_params=GRANT,
    )(scales, d_gate, d_up, w_gate, w_up)


def layer(tokens, expert_ids, route_probs, scale_exps, w_gate, w_up, w_down, out_grad):
    scales = jnp.exp2(scale_exps.astype(F32))
    combine = jnp.sum(jnp.where(expert_ids == 0, route_probs, jnp.zeros_like(route_probs)), axis=1)[
        :, None
    ]
    table = jnp.asarray(place_table())[lax.axis_index("dp")]
    scaled = (combine * out_grad.astype(F32)).astype(BF16)
    w_gate_now, w_up_now = load(w_gate)[0], load(w_up)[0]
    w_gate, w_up, w_down = (
        pltpu.with_memory_space_constraint(w, pltpu.VMEM) for w in (w_gate, w_up, w_down)
    )
    token_pieces = gather_blk(tokens)
    scaled_pieces = gather_blk(scaled)
    all_tokens, hidden, to_gate, to_up = forward(scales, token_pieces, w_gate_now, w_up_now)
    all_scaled, send_a, keep_a, send_b, keep_b = wgrad_join(table, hidden, scaled_pieces)
    later, combine_later, send_a = lax.optimization_barrier((hidden, combine, send_a))
    grad_down = scatter_dp_x((send_a, keep_a, send_b, keep_b), table, scales, 2, False)

    d_gate, d_up = backward(scales, all_scaled, w_down, to_gate, to_up)
    grad_gate = scatter_dp_y(wgrad_y(table, d_gate, all_tokens), scales, 0, True)
    send_a, keep_a, send_b, keep_b = wgrad_x(table, d_up, all_tokens)
    grad_up = scatter_dp_x((send_a, keep_a, send_b, keep_b), table, scales, 1, True)

    other, own = down(later, w_down)
    expert_out = scatter_blk(own, other) * scales[2]
    mixed = (combine_later * expert_out).astype(BF16)
    other, own = back(scales, d_gate, d_up, w_gate, w_up)
    input_grad = scatter_blk(own, other)
    return (
        mixed,
        input_grad.astype(BF16),
        grad_gate,
        grad_up,
        grad_down,
    )


def solution(mesh):
    return jax.shard_map(
        layer,
        mesh=mesh,
        in_specs=(
            P(("dp", "blk"), None),
            P(("dp", "blk"), None),
            P(("dp", "blk"), None),
            P(),
            P(None, "blk"),
            P(None, "blk"),
            P("blk", None),
            P(("dp", "blk"), None),
        ),
        out_specs=(
            P(("dp", "blk"), None),
            P(("dp", "blk"), None),
            P("dp", "blk"),
            P("dp", "blk"),
            P("blk", "dp"),
        ),
        check_vma=False,
    )
```
